256 devices in a mesh: prow: 8 (over z), pcol: 32 (over x, y, core).
Axes of the slice: x: 4, y: 4, z: 8, core: 2. Of those that a mesh axis runs over, the one named last changes fastest.
Arguments:
- b_panels: bfloat16 [3, 8, 32, 128, 512], P(None, 'prow', 'pcol'), may hold values from -6 to 6
- diag_inverse: bfloat16 [3, 8, 32, 128, 128], P(None, 'prow', 'pcol'), as said below
- l_blocks: bfloat16 [2, 8, 32, 32, 5, 128, 128], P(None, 'prow', 'pcol'), may hold values from -0.0390625 to 0.0390625
- block_cols: int32 [2, 8, 32, 32, 5], P(None, 'prow', 'pcol'), may hold values from 0 to 511, as said below
- live_counts: int32 [2, 8, 32, 32], P(None, 'prow', 'pcol'), may hold values from 0 to 5, as said below
Outputs:
- solution: bfloat16 [3, 8, 32, 128, 512], P(None, 'prow', 'pcol')
The draws below stay inside these ranges and needn't reach their ends.
Inputs may be any that keep to these rules, and one draw needn't show every extreme that they name: `block_cols`: for block row (l, r, q) and device column c, entries are l2 * 256 + p * 32 + c with l2 < l and 0 <= p < 8; the first live_counts[l - 1, r, c, q] slots are distinct. `live_counts`: at most min(5, l * 8) at level l; that bound is reached at every level. `diag_inverse`: lower triangular.
All inputs are finite; a program needn't handle non-finite values.
Results may differ from the reference program's by a relative error of at most 0.014.
Values may be sent and summed in bfloat16 or wider, within the bound.
A program may use at most 128 MiB of HBM per device.

```python
import math
import jax
import jax.numpy as jnp
from jax import lax

B = 128
RHS = 512
LEVELS = 3
BLOCK_SLOT_COUNT = 5
NB_LEV = 256
N_PROW = 8
N_PCOL = 32


def draw_diag_inverse(key, part):
    first_key, secondary_key = jax.random.split(key)
    shape = (LEVELS, N_PROW, N_PCOL, B, B)
    lower_part = jax.random.normal(first_key, shape, jnp.float32) * (0.6 / math.sqrt(B))
    diagonal = jax.random.uniform(secondary_key, shape[:-1], jnp.float32, 0.7, 1.3)
    row_pos = jnp.arange(B)[:, None]
    col_pos = jnp.arange(B)[None, :]
    strict = jnp.where(row_pos > col_pos, lower_part, 0.0)
    return (strict + jnp.where(row_pos == col_pos, diagonal[..., :, None], 0.0)).astype(jnp.bfloat16)


def draw_block_cols(key, part):
    candidates = (LEVELS - 1) * N_PROW
    randomness_words = jax.random.randint(jax.random.fold_in(key, 11), (LEVELS - 1, N_PROW, N_PCOL, N_PCOL, candidates), 0, 1 << 20)
    candidate = jnp.arange(candidates).astype(jnp.int32)
    level_lookup = jnp.arange(1, LEVELS).astype(jnp.int32)[:, None, None, None, None]
    valid = candidate < level_lookup * N_PROW
    scores = jnp.where(valid, randomness_words * candidates + candidate, -1 - candidate)
    _, chosen = lax.top_k(scores, BLOCK_SLOT_COUNT)
    chosen = jnp.minimum(chosen.astype(jnp.int32), level_lookup * N_PROW - 1)
    prior_level = chosen // N_PROW
    prior_slot = chosen % N_PROW
    col_owner = jnp.arange(N_PCOL).astype(jnp.int32)[None, None, :, None, None]
    return (prior_level * NB_LEV + prior_slot * N_PCOL + col_owner).astype(jnp.int32)


def draw_live_counts(key, part):
    first_key, secondary_key = jax.random.split(jax.random.fold_in(key, 7))
    baseline_workload = jax.random.randint(first_key, (LEVELS - 1, N_PROW, N_PCOL, N_PCOL), 0, BLOCK_SLOT_COUNT + 1)
    column_extra_reward = jax.random.randint(secondary_key, (1, 1, N_PCOL, 1), 0, BLOCK_SLOT_COUNT)
    level_ceiling = jnp.minimum(BLOCK_SLOT_COUNT, jnp.arange(1, LEVELS).astype(jnp.int32) * N_PROW)[:, None, None, None]
    currently_active = jnp.minimum(jnp.minimum(baseline_workload + column_extra_reward, BLOCK_SLOT_COUNT), level_ceiling)
    currently_active = currently_active.at[:, 0, 0, 0].set(level_ceiling[:, 0, 0, 0])
    return currently_active.astype(jnp.int32)


def block_scale(key, extent, shards, least, largest):
    loudness, own = 1.0, jax.random.fold_in(key, 6)
    for axis_at, blocks in shards:
        draws = jnp.exp(jax.random.uniform(jax.random.fold_in(own, axis_at), (blocks,), jnp.float32, least / len(shards), largest / len(shards)))
        loudness = loudness * jnp.repeat(draws, extent[axis_at] // blocks).reshape([-1 if axis == axis_at else 1 for axis in range(len(extent))])
    return loudness


def centred(stream_key, shape, width, reach, cuts=(), held_as=jnp.bfloat16):
    result = jax.random.normal(stream_key, shape, jnp.float32) * width
    if len(cuts) > 0:
        result = block_scale(stream_key, shape, cuts, -0.22, 0.18) * result
    return jnp.clip(result, min=-reach, max=reach).astype(held_as)


def setup_inputs(seed: int = 0) -> dict:
    splits = jax.random.split(jax.random.key(seed), 6)
    b_panels = centred(splits[0], (LEVELS, N_PROW, N_PCOL, B, RHS), 1.0, 6.0, ((1, 8), (2, 32)))
    diag_inverse = draw_diag_inverse(jax.random.fold_in(splits[5], 71), 0)
    l_blocks = centred(splits[2], (LEVELS - 1, N_PROW, N_PCOL, N_PCOL, BLOCK_SLOT_COUNT, B, B), (B * N_PCOL * BLOCK_SLOT_COUNT) ** -0.5, 0.0390625, ((1, 8), (2, 32)))
    block_cols = draw_block_cols(jax.random.fold_in(splits[5], 71), 0)
    live_counts = draw_live_counts(jax.random.fold_in(splits[5], 71), 0)
    return dict(b_panels=b_panels, diag_inverse=diag_inverse, l_blocks=l_blocks, block_cols=block_cols, live_counts=live_counts)


def reference(b_panels, diag_inverse, l_blocks, block_cols, live_counts):
    proc_rows = N_PROW
    proc_cols = N_PCOL
    per_level = proc_rows * proc_cols
    solved = jnp.zeros((LEVELS * per_level, B, RHS), jnp.bfloat16)
    solutions = []
    for level_idx in range(LEVELS):
        right_part = b_panels[level_idx].astype(jnp.float32)
        if level_idx > 0:
            blocks = l_blocks[level_idx - 1]
            chosen = block_cols[level_idx - 1]
            currently_active = live_counts[level_idx - 1]

            def process_row(row_idx):
                def add_column(row_total, col_idx):
                    slot_mask = jnp.arange(BLOCK_SLOT_COUNT)[None, :] < currently_active[row_idx, col_idx][:, None]
                    masked = jnp.where(slot_mask[:, :, None, None], blocks[row_idx, col_idx], jnp.zeros((), jnp.bfloat16))
                    fetched = solved[chosen[row_idx, col_idx].astype(jnp.int32)].astype(jnp.float32)
                    partial_sum = jnp.einsum("jkab,jkbr->jar", masked.astype(jnp.float32), fetched,
                                             precision=lax.Precision.HIGHEST)
                    rounded = lax.optimization_barrier(partial_sum.astype(jnp.bfloat16))
                    return row_total + rounded.astype(jnp.float32), None

                start_total = jnp.zeros((proc_cols, B, RHS), jnp.float32)
                row_total, _ = lax.scan(add_column, start_total, jnp.arange(proc_cols).astype(jnp.int32))
                return row_total

            sums = lax.map(process_row, jnp.arange(proc_rows).astype(jnp.int32))
            right_part = right_part - sums
        resid = right_part.astype(jnp.bfloat16)
        solution = jnp.einsum("rcab,rcbs->rcas", diag_inverse[level_idx].astype(jnp.float32),
                              resid.astype(jnp.float32), precision=lax.Precision.HIGHEST).astype(jnp.bfloat16)
        solved = solved.at[level_idx * per_level:(level_idx + 1) * per_level].set(
            solution.reshape(per_level, B, RHS))
        solutions.append(solution)
    return jnp.stack(solutions)
```

```python
import functools

import jax
import jax.numpy as jnp
from jax import lax
from jax.experimental import pallas as pl
from jax.experimental.pallas import tpu as pltpu
from jax.sharding import Mesh
from jax.sharding import PartitionSpec as P

PCOL = ("pcol_0", "pcol_1", "pcol_2")
CHUNKS = 2
B = 128
RHS = 512
W = RHS // CHUNKS
SLOTS = 5
NZ = 8
HALF = B // 2
QUARTER = B // 4
COPIES = CHUNKS * 2 * (8 + 4 + 12 + 12)
ORDER = ()


def kernel(
    cols, live, b_hbm, d_hbm, l_hbm, out,
    lv, bv, dv, xs, ps, pr, sums, r1, mid, r2, resid,
    in_sem, ssem, rsem, credit,
):
    z = lax.axis_index("prow")
    x = lax.axis_index("pcol_0")
    y = lax.axis_index("pcol_1")
    c = lax.axis_index("pcol_2")
    mate = 1 - c
    away = (("pcol_0", x), ("pcol_1", y))

    def turn(value, step, size):
        return lax.rem(value + (step + size), size)

    loads = {}
    waited = set()

    def load(name, src, dst):
        loads[name] = pltpu.make_async_copy(src, dst, in_sem.at[len(loads)])
        loads[name].start()

    load("d", d_hbm, dv)
    load("b", b_hbm, bv)
    load("l0", l_hbm.at[0], lv.at[0])
    load("l1", l_hbm.at[1], lv.at[1])

    barrier = pltpu.get_barrier_semaphore()
    friends = [{"pcol_2": mate}]
    for axis, value, size in (("pcol_0", x, 4), ("pcol_1", y, 4), ("prow", z, NZ)):
        for step in (1, -1):
            friends.append({axis: turn(value, step, size)})
    for friend in friends:
        pl.semaphore_signal(barrier, inc=1, device_id=friend, device_id_type=pl.DeviceIdType.MESH)

    count = [0]
    started = []

    def send(src, dst, friend):
        at = count[0]
        count[0] += 1
        copy = pltpu.make_async_remote_copy(
            src_ref=src, dst_ref=dst, send_sem=ssem.at[at], recv_sem=rsem.at[at],
            device_id=friend, device_id_type=pl.DeviceIdType.MESH,
        )
        copy.start()
        started.append(copy)
        return copy

    def gather(g, level):
        held = xs[g]
        base = level * NZ
        if level > 0:
            pl.semaphore_wait(credit.at[g, 0], 1)
            pl.semaphore_wait(credit.at[g, 1], 1)
        last = [None, None]
        for step in range(4):
            for d, sign in enumerate((1, -1)):
                if last[d] is not None:
                    last[d].wait_recv()
                slot = held.at[base + turn(z, -sign * step, NZ)]
                if step == 3:
                    slot = slot.at[pl.ds(d * HALF, HALF)]
                last[d] = send(slot, slot, {"prow": turn(z, sign, NZ)})
            yield
        last[0].wait_recv()
        last[1].wait_recv()

    def row_total(g, level, q):
        held = xs[g]
        lefts, rights = [], []
        for k in range(SLOTS):
            v = cols[level, q, k]
            at = (v // 256) * NZ + (v % 256) // 32
            rights.append(held[jnp.where(k < live[level, q], at, 2 * NZ)])
            lefts.append(lv[level, q, k])
        return jnp.dot(
            jnp.concatenate(lefts, axis=1), jnp.concatenate(rights, axis=0),
            preferred_element_type=jnp.float32,
        )

    def products(g, level):
        if level not in waited:
            waited.add(level)
            loads["l%d" % level].wait()
        total = sums.at[level, g]
        pair = [None] * 4
        offsets = (2, 1, -1, 0)
        pending = []

        def theirs(n):
            xd = turn(x, offsets[n], 4)
            for j in range(4):
                q = (xd * 4 + j) * 2 + mate
                ps[level, g, xd, j] = row_total(g, level, q).astype(jnp.bfloat16)
            pair[n] = send(ps.at[level, g, xd], pr.at[level, g, xd], {"pcol_2": mate})

        def ours(n):
            xd = turn(x, offsets[n], 4)
            pair[n].wait_recv()
            for j in range(4):
                q = (xd * 4 + j) * 2 + c
                row = row_total(g, level, q) + pr[level, g, xd, j].astype(jnp.float32)
                total[xd, j] = row.astype(jnp.bfloat16)
        theirs(0)
        for n in range(1, 5):
            if n < 4:
                theirs(n)
            ours(n - 1)
            yield

    def ring(blocks, landing, axis, value, kind, copies, d):
        sign = 1 - 2 * d
        to = {axis: turn(value, sign, 4)}
        if kind == 0:
            src = blocks(turn(value, 2, 4), d)
        elif kind == 1:
            src = blocks(turn(value, sign, 4), 1 - d)
        else:
            copies[d, 0].wait_recv()
            mine = blocks(turn(value, sign, 4), d)
            mine[...] = mine[...] + landing.at[d, 0][...]
            src = mine
        copies[d, kind] = send(src, landing.at[d, kind], to)

    def exchange(g, level):
        total = sums.at[level, g]
        axes = (("pcol_0", x), ("pcol_1", y))

        def first(o):
            def blocks(dest, piece):
                if o == 0:
                    return total.at[dest, pl.ds(2 * piece, 2), pl.ds(0, HALF)]
                return total.at[pl.ds(2 * piece, 2), dest, pl.ds(HALF, HALF)]
            return blocks

        def second(o):
            def blocks(dest, piece):
                return mid.at[level, g, o, dest, pl.ds(QUARTER * piece, QUARTER)]
            return blocks

        one = [{}, {}]
        two = [{}, {}]
        for kind in (0, 1):
            for o in range(2):
                for d in range(2):
                    ring(first(o), r1.at[level, g, o], *axes[o], kind, one[o], d)
        yield
        for o in range(2):
            for d in range(2):
                ring(first(o), r1.at[level, g, o], *axes[o], 2, one[o], d)
        yield
        for o in range(2):
            own = axes[o][1]
            for p in range(2):
                one[o][1 - p, 1].wait_recv()
                one[o][p, 2].wait_recv()
                mine = first(o)(own, p)[...].astype(jnp.float32)
                mine = mine + r1[level, g, o, 1 - p, 1].astype(jnp.float32)
                mine = mine + r1[level, g, o, p, 2].astype(jnp.float32)
                mid[level, g, o, pl.ds(2 * p, 2)] = mine.astype(jnp.bfloat16)
            for kind in (0, 1):
                for d in range(2):
                    ring(second(o), r2.at[level, g, o], *axes[1 - o], kind, two[o], d)
        yield
        for o in range(2):
            for d in range(2):
                ring(second(o), r2.at[level, g, o], *axes[1 - o], 2, two[o], d)
        yield
        for o in range(2):
            own = axes[1 - o][1]
            for p in range(2):
                two[o][1 - p, 1].wait_recv()
                two[o][p, 2].wait_recv()
                mine = second(o)(own, p)[...].astype(jnp.float32)
                mine = mine + r2[level, g, o, 1 - p, 1].astype(jnp.float32)
                mine = mine + r2[level, g, o, p, 2].astype(jnp.float32)
                rows = pl.ds(o * HALF + p * QUARTER, QUARTER)
                right = bv[level + 1, 0, 0, rows, pl.ds(g * W, W)].astype(jnp.float32)
                resid[g, rows] = (right - mine).astype(jnp.bfloat16)

    def solve(g, level, right):
        answer = jnp.dot(
            dv[level, 0, 0], right, preferred_element_type=jnp.float32
        ).astype(jnp.bfloat16)
        out[level, 0, 0, :, pl.ds(g * W, W)] = answer
        if level < 2:
            xs[g][level * NZ + z] = answer

    def chunk(g):
        xs[g][2 * NZ] = jnp.zeros((B, W), jnp.bfloat16)
        solve(g, 0, bv[0, 0, 0, :, pl.ds(g * W, W)])
        if g == 0:
            pl.semaphore_wait(barrier, len(friends))
        for level in range(2):
            yield from gather(g, level)
            yield from products(g, level)
            if level == 0:
                for i, sign in enumerate((1, -1)):
                    pl.semaphore_signal(
                        credit.at[g, i], inc=1, device_id={"prow": turn(z, sign, NZ)},
                        device_id_type=pl.DeviceIdType.MESH,
                    )
            yield from exchange(g, level)
            solve(g, level + 1, resid[g])

    loads["d"].wait()
    loads["b"].wait()
    running = [chunk(g) for g in range(CHUNKS)]
    alive = set(range(CHUNKS))

    def advance(g):
        if g in alive and next(running[g], "end") == "end":
            alive.discard(g)

    for g in ORDER:
        advance(g)
    while alive:
        for g in sorted(alive):
            advance(g)
    for copy in started:
        copy.wait_send()


def shards(b_panels, diag_inverse, l_blocks, block_cols, live_counts):
    any_spec = pl.BlockSpec(memory_space=pl.ANY)
    smem = pl.BlockSpec(memory_space=pltpu.SMEM)
    bf16 = jnp.bfloat16
    return pl.pallas_call(
        kernel,
        name="front",
        out_shape=jax.ShapeDtypeStruct(b_panels.shape, bf16),
        in_specs=[smem, smem, any_spec, any_spec, any_spec],
        out_specs=pl.BlockSpec(memory_space=pltpu.VMEM),
        scratch_shapes=[
            pltpu.VMEM((2, 32, SLOTS, B, B), bf16),
            pltpu.VMEM(b_panels.shape, bf16),
            pltpu.VMEM(diag_inverse.shape, bf16),
            [pltpu.VMEM((2 * NZ + 1, B, W), bf16) for _ in range(CHUNKS)],
            pltpu.VMEM((2, CHUNKS, 4, 4, B, W), bf16),
            pltpu.VMEM((2, CHUNKS, 4, 4, B, W), bf16),
            pltpu.VMEM((2, CHUNKS, 4, 4, B, W), bf16),
            pltpu.VMEM((2, CHUNKS, 2, 2, 3, 2, HALF, W), bf16),
            pltpu.VMEM((2, CHUNKS, 2, 4, HALF, W), bf16),
            pltpu.VMEM((2, CHUNKS, 2, 2, 3, QUARTER, W), bf16),
            pltpu.VMEM((CHUNKS, B, W), bf16),
            pltpu.SemaphoreType.DMA((4,)),
            pltpu.SemaphoreType.DMA((COPIES,)),
            pltpu.SemaphoreType.DMA((COPIES,)),
            pltpu.SemaphoreType.REGULAR((CHUNKS, 2)),
        ],
        compiler_params=pltpu.CompilerParams(
            collective_id=0, has_side_effects=True, vmem_limit_bytes=60 * 2**20
        ),
    )(
        block_cols.reshape(2, 32, SLOTS),
        live_counts.reshape(2, 32),
        b_panels,
        diag_inverse,
        l_blocks.reshape(2, 32, SLOTS, B, B),
    )


def solution(mesh):
    finer = Mesh(
        mesh.devices.reshape(mesh.shape["prow"], 4, 4, 2), ("prow", "pcol_0", "pcol_1", "pcol_2")
    )
    return jax.shard_map(
        shards,
        mesh=finer,
        in_specs=(
            P(None, "prow", PCOL, None, None),
            P(None, "prow", PCOL, None, None),
            P(None, "prow", PCOL, None, None, None, None),
            P(None, "prow", PCOL, None, None),
            P(None, "prow", PCOL, None),
        ),
        out_specs=P(None, "prow", PCOL, None, None),
        check_vma=False,
    )
```

```python
import functools

import jax
import jax.numpy as jnp
from jax import lax
from jax.experimental import pallas as pl
from jax.experimental.pallas import tpu as pltpu
from jax.sharding import Mesh
from jax.sharding import PartitionSpec as P

PCOL = ("pcol_0", "pcol_1", "pcol_2")
CHUNKS = 2
B = 128
RHS = 512
W = RHS // CHUNKS
SLOTS = 5
NZ = 8
HALF = B // 2
PIECES = 4
PIECE = B // PIECES
SIGN = (1, -1)
NEAR = (1, 3)
VIA = ((2, 1), (0, 3))
GROUPS = (
    ((2, 2), (2, 0), (0, 2), (2, 1)),
    ((1, 2), (2, 3), (3, 2), (1, 1)),
    ((3, 3), (1, 3), (3, 1), (1, 0)),
    ((0, 1), (3, 0), (0, 3), (0, 0)),
)
ORDER = (
    0, 75, 3, 1, 2, 77, 4, 79, 78, 76, 7, 5, 6, 8, 83, 82, 11, 81, 80, 9, 10, 12, 84, 86, 85,
    87, 13, 14, 15, 16, 17, 18, 19, 88, 20, 31, 21, 89, 22, 29, 24, 23, 30, 32, 92, 90, 91, 33,
    27, 35, 26, 36, 28, 34, 93, 104, 96, 94, 95, 98, 25, 106, 37, 105, 97, 107, 102, 99, 110,
    108, 38, 101, 39, 109, 40, 111, 103, 41, 100, 43, 44, 42, 45, 112, 48, 46, 49, 47, 113, 115,
    116, 114, 50, 51, 117, 52, 120, 118, 119, 53, 54, 55, 121, 124, 56, 122, 123, 58, 66, 57,
    60, 67, 59, 61, 68, 125, 126, 69, 127, 64, 72, 129, 130, 131, 65, 128, 133, 141, 142, 136,
    134, 132, 144, 73, 70, 71, 147, 63, 143, 146, 135, 139, 140, 62, 148, 138, 145, 74, 137,
    149,
)


def goes(step, d):
    if step < 3:
        return tuple(range(PIECES))
    return tuple(h for h in range(PIECES) if h * 2 // PIECES == d)


def plan(g):
    steps = {}
    for lv in range(2):
        after = [] if lv == 0 else [("settle", g, 0, o, r) for o in range(2) for r in range(4)]
        got = [] if lv == 0 else [("two", g, 0, o, r) for o in range(2) for r in (1, 2, 3)]
        sent = [("ag", g, lv, 0, d, h) for h in range(PIECES) for d in range(2)]
        steps["solve", g, lv] = (after, got, sent)
        for step in (1, 2, 3):
            for h in range(PIECES):
                ds = [d for d in range(2) if h in goes(step, d)]
                steps["ag", g, lv, step, h] = (
                    [("solve", g, lv)],
                    [("ag", g, lv, step - 1, d, h) for d in ds],
                    [("ag", g, lv, step, d, h) for d in ds],
                )
        last = [("ag", g, lv, 3, d, h) for d in range(2) for h in goes(3, d)]
        last += [
            ("ag", g, lv, 2, d, h) for d in range(2) for h in range(PIECES) if h not in goes(3, d)
        ]
        for n in range(4):
            before = [("theirs", g, lv, n - 1)] if n else [
                ("ag", g, lv, step, h) for step in (1, 2, 3) for h in range(PIECES)
            ]
            steps["theirs", g, lv, n] = (before, [] if n else last, [("pair", g, lv, n)])
        where = {}
        for n in range(4):
            sent = []
            for row in GROUPS[n]:
                where[row] = n
                for o in range(2):
                    main, r = (row[0], row[1]) if o == 0 else (row[1], row[0])
                    for d in range(2):
                        if main == 2 and r in VIA[d]:
                            sent.append(("far", g, lv, o, d, r))
                        if main == NEAR[d] and r not in VIA[d]:
                            sent.append(("near", g, lv, o, d, r))
            before = [("theirs", g, lv, n)] + ([("ours", g, lv, n - 1)] if n else [])
            steps["ours", g, lv, n] = (before, [("pair", g, lv, n)], sent)
        for o in range(2):
            for d in range(2):
                for r in VIA[d]:
                    row = (NEAR[d], r) if o == 0 else (r, NEAR[d])
                    steps["relay", g, lv, o, d, r] = (
                        [("ours", g, lv, where[row])],
                        [("far", g, lv, o, d, r)],
                        [("near", g, lv, o, d, r)],
                    )
            for r in range(4):
                row = (0, r) if o == 0 else (r, 0)
                steps["settle", g, lv, o, r] = (
                    [("ours", g, lv, where[row])],
                    [("near", g, lv, o, d, r) for d in range(2)],
                    [("two", g, lv, o, r)] if r else [],
                )
    steps["solve", g, 2] = (
        [("settle", g, 1, o, r) for o in range(2) for r in range(4)],
        [("two", g, 1, o, r) for o in range(2) for r in (1, 2, 3)],
        [],
    )
    return steps


def messages():
    return {
        name: at
        for at, name in enumerate(m for g in range(CHUNKS) for s in plan(g).values() for m in s[2])
    }


def kernel(
    cols, live, b_hbm, d_hbm, l_hbm, out,
    lv_ref, bv, dv, xs, ps, pr, sums, far, near, mid, two, resid,
    in_sem, ssem, rsem, credit,
):
    z = lax.axis_index("prow")
    x = lax.axis_index("pcol_0")
    y = lax.axis_index("pcol_1")
    c = lax.axis_index("pcol_2")
    mate = 1 - c
    grid = ("pcol_0", "pcol_1")
    mesh_id = pl.DeviceIdType.MESH

    here = {"prow": z, "pcol_0": x, "pcol_1": y, "pcol_2": c}
    turned = {
        axis: [value] + [lax.rem(value + k, size) for k in range(1, size)]
        for axis, value, size in (("prow", z, NZ), ("pcol_0", x, 4), ("pcol_1", y, 4))
    }

    def turn(axis, step):
        return turned[axis][step % len(turned[axis])]

    def at_device(axis, value):
        return tuple(value if name == axis else here[name] for name in here)

    loads = {}

    def load(name, src, dst):
        loads[name] = pltpu.make_async_copy(src, dst, in_sem.at[len(loads)])
        loads[name].start()

    load("d", d_hbm, dv)
    load("b", b_hbm, bv)
    load("l0", l_hbm.at[0], lv_ref.at[0])
    load("l1", l_hbm.at[1], lv_ref.at[1])

    barrier = pltpu.get_barrier_semaphore()
    friends = [at_device("pcol_2", mate)]
    friends += [at_device(axis, turn(axis, step)) for axis in grid for step in (1, 2, 3)]
    friends += [at_device("prow", turn("prow", sign)) for sign in SIGN]
    for friend in friends:
        pl.semaphore_signal(barrier, inc=1, device_id=friend, device_id_type=mesh_id)

    number = messages()
    copies = {}

    def half(lv, g, o, main, r):
        rx, ry = (main, r) if o == 0 else (r, main)
        return sums.at[lv, g, rx, ry, pl.ds(o * HALF, HALF)]

    def ends(name):
        kind, g, lv = name[:3]
        if kind == "ag":
            step, d, h = name[3:]
            slot = xs[g].at[
                lv * NZ + turn("prow", -SIGN[d] * step), pl.ds(h * PIECE, PIECE)
            ]
            return slot, slot, at_device("prow", turn("prow", SIGN[d]))
        if kind == "pair":
            n = name[3]
            return ps.at[lv, g, n], pr.at[lv, g, n], at_device("pcol_2", mate)
        if kind == "two":
            o, r = name[3:]
            axis = grid[1 - o]
            friend = at_device(axis, turn(axis, r))
            return mid.at[lv, g, o, r], two.at[lv, g, o, r - 1], friend
        o, d, r = name[3:]
        axis = grid[o]
        friend = at_device(axis, turn(axis, SIGN[d]))
        if kind == "far":
            return half(lv, g, o, 2, r), far.at[lv, g, o, d, VIA[d].index(r)], friend
        return half(lv, g, o, NEAR[d], r), near.at[lv, g, o, d, r], friend

    def send(name):
        src, dst, friend = ends(name)
        at = number[name]
        copies[name] = pltpu.make_async_remote_copy(
            src_ref=src, dst_ref=dst, send_sem=ssem.at[at], recv_sem=rsem.at[at],
            device_id=friend, device_id_type=mesh_id,
        )
        copies[name].start()

    def row_total(g, lv, q):
        lefts, rights = [], []
        for k in range(SLOTS):
            v = cols[lv * SLOTS + k, 0, q]
            at = (v >> 8) * NZ + ((v & 255) >> 5)
            rights.append(xs[g][jnp.where(k < live[lv, q], at, 2 * NZ)])
            lefts.append(lv_ref[lv, q, k])
        return jnp.dot(
            jnp.concatenate(lefts, axis=1), jnp.concatenate(rights, axis=0),
            preferred_element_type=jnp.float32,
        )

    def row_of(row, core):
        return (turn("pcol_0", row[0]) * 4 + turn("pcol_1", row[1])) * 2 + core

    def f32(value):
        return value.astype(jnp.float32)

    def do(name):
        kind, g, lv = name[:3]
        if kind == "solve":
            here = pl.ds(g * W, W)
            if lv == 0:
                right = bv[0, 0, 0, :, here]
                xs[g][2 * NZ] = jnp.zeros((B, W), jnp.bfloat16)
            else:
                for o in range(2):
                    total = f32(mid[lv - 1, g, o, 0])
                    for r in range(3):
                        total = total + f32(two[lv - 1, g, o, r])
                    rows = pl.ds(o * HALF, HALF)
                    resid[g, rows] = (f32(bv[lv, 0, 0, rows, here]) - total).astype(jnp.bfloat16)
                right = resid[g]
            answer = jnp.dot(
                dv[lv, 0, 0], right, preferred_element_type=jnp.float32
            ).astype(jnp.bfloat16)
            out[lv, 0, 0, :, here] = answer
            if lv < 2:
                xs[g][lv * NZ + z] = answer
            if lv == 0 and "barrier" not in loads:
                loads["barrier"] = None
                pl.semaphore_wait(barrier, len(friends))
            if lv == 1:
                for i in range(2):
                    pl.semaphore_wait(credit.at[g, i], 1)
        elif kind == "theirs":
            if loads["l%d" % lv] is not None:
                loads["l%d" % lv].wait()
                loads["l%d" % lv] = None
            n = name[3]
            for i, row in enumerate(GROUPS[n]):
                ps[lv, g, n, i] = row_total(g, lv, row_of(row, mate)).astype(jnp.bfloat16)
        elif kind == "ours":
            n = name[3]
            for i, row in enumerate(GROUPS[n]):
                total = row_total(g, lv, row_of(row, c)) + f32(pr[lv, g, n, i])
                sums[lv, g, row[0], row[1]] = total.astype(jnp.bfloat16)
            if n == 3 and lv == 0:
                for i, sign in enumerate(SIGN):
                    pl.semaphore_signal(
                        credit.at[g, i], inc=1, device_id_type=mesh_id,
                        device_id=at_device("prow", turn("prow", sign)),
                    )
        elif kind == "relay":
            o, d, r = name[3:]
            mine = half(lv, g, o, NEAR[d], r)
            mine[...] = mine[...] + far[lv, g, o, d, VIA[d].index(r)]
        elif kind == "settle":
            o, r = name[3:]
            total = f32(half(lv, g, o, 0, r)[...])
            total = total + f32(near[lv, g, o, 0, r]) + f32(near[lv, g, o, 1, r])
            mid[lv, g, o, r] = total.astype(jnp.bfloat16)

    loads["d"].wait()
    loads["b"].wait()
    steps = {}
    for g in range(CHUNKS):
        steps.update(plan(g))
    names = list(steps)
    for at in ORDER:
        name = names[at]
        for message in steps[name][1]:
            copies[message].wait_recv()
        do(name)
        for message in steps[name][2]:
            send(message)
    for copy in copies.values():
        copy.wait_send()


def shards(b_panels, diag_inverse, l_blocks, block_cols, live_counts):
    any_spec = pl.BlockSpec(memory_space=pl.ANY)
    smem = pl.BlockSpec(memory_space=pltpu.SMEM)
    bf16 = jnp.bfloat16
    count = len(messages())
    return pl.pallas_call(
        kernel,
        name="front",
        out_shape=jax.ShapeDtypeStruct(b_panels.shape, bf16),
        in_specs=[smem, smem, any_spec, any_spec, any_spec],
        out_specs=pl.BlockSpec(memory_space=pltpu.VMEM),
        scratch_shapes=[
            pltpu.VMEM((2, 32, SLOTS, B, B), bf16),
            pltpu.VMEM(b_panels.shape, bf16),
            pltpu.VMEM(diag_inverse.shape, bf16),
            [pltpu.VMEM((2 * NZ + 1, B, W), bf16) for _ in range(CHUNKS)],
            pltpu.VMEM((2, CHUNKS, 4, 4, B, W), bf16),
            pltpu.VMEM((2, CHUNKS, 4, 4, B, W), bf16),
            pltpu.VMEM((2, CHUNKS, 4, 4, B, W), bf16),
            pltpu.VMEM((2, CHUNKS, 2, 2, 2, HALF, W), bf16),
            pltpu.VMEM((2, CHUNKS, 2, 2, 4, HALF, W), bf16),
            pltpu.VMEM((2, CHUNKS, 2, 4, HALF, W), bf16),
            pltpu.VMEM((2, CHUNKS, 2, 3, HALF, W), bf16),
            pltpu.VMEM((CHUNKS, B, W), bf16),
            pltpu.SemaphoreType.DMA((4,)),
            pltpu.SemaphoreType.DMA((count,)),
            pltpu.SemaphoreType.DMA((count,)),
            pltpu.SemaphoreType.REGULAR((CHUNKS, 2)),
        ],
        compiler_params=pltpu.CompilerParams(
            collective_id=0, has_side_effects=True, vmem_limit_bytes=60 * 2**20
        ),
    )(
        block_cols.transpose(0, 1, 4, 2, 3).reshape(2 * SLOTS, 1, 32),
        live_counts.reshape(2, 32),
        b_panels,
        diag_inverse,
        l_blocks.reshape(2, 32, SLOTS, B, B),
    )


def solution(mesh):
    finer = Mesh(
        mesh.devices.reshape(mesh.shape["prow"], 4, 4, 2), ("prow", "pcol_0", "pcol_1", "pcol_2")
    )
    return jax.shard_map(
        shards,
        mesh=finer,
        in_specs=(
            P(None, "prow", PCOL, None, None),
            P(None, "prow", PCOL, None, None),
            P(None, "prow", PCOL, None, None, None, None),
            P(None, "prow", PCOL, None, None),
            P(None, "prow", PCOL, None),
        ),
        out_specs=P(None, "prow", PCOL, None, None),
        check_vma=False,
    )
```

```python
import functools

import jax
import jax.numpy as jnp
from jax import lax
from jax.experimental import pallas as pl
from jax.experimental.pallas import tpu as pltpu
from jax.sharding import Mesh
from jax.sharding import PartitionSpec as P

PCOL = ("pcol_0", "pcol_1", "pcol_2")
CHUNKS = 2
B = 128
RHS = 512
W = RHS // CHUNKS
SLOTS = 5
NZ = 8
HALF = B // 2
PIECES = 2
PIECE = B // PIECES
SIGN = (1, -1)
NEAR = (1, 3)
VIA = ((2, 1), (0, 3))
GROUPS = (
    ((2, 2), (2, 0), (0, 2), (2, 1)),
    ((1, 2), (2, 3), (3, 2), (1, 1)),
    ((3, 3), (1, 3), (3, 1), (1, 0)),
    ((0, 1), (3, 0), (0, 3), (0, 0)),
)
ORDER = (
    0, 71, 2, 1, 4, 3, 73, 72, 75, 74, 6, 5, 8, 7, 77, 76, 79, 78, 9, 10, 80, 81, 11, 12, 13,
    82, 83, 84, 15, 16, 86, 87, 19, 17, 20, 27, 14, 90, 28, 22, 30, 88, 98, 85, 91, 99, 93, 101,
    25, 33, 18, 29, 21, 24, 32, 26, 34, 96, 104, 89, 92, 100, 103, 95, 97, 105, 23, 31, 35, 94,
    102, 106, 37, 36, 39, 38, 108, 107, 110, 109, 41, 40, 43, 42, 112, 111, 114, 113, 44, 45,
    115, 116, 46, 47, 48, 117, 118, 50, 51, 121, 122, 119, 62, 54, 52, 49, 55, 63, 57, 65, 133,
    125, 120, 123, 128, 126, 60, 68, 53, 136, 56, 64, 134, 67, 59, 61, 69, 131, 139, 124, 127,
    135, 130, 138, 132, 140, 58, 66, 70, 129, 137, 141,
)


def goes(step, d):
    if step < 3:
        return tuple(range(PIECES))
    return tuple(h for h in range(PIECES) if h * 2 // PIECES == d)


def plan(g):
    steps = {}
    for lv in range(2):
        after = [] if lv == 0 else [("settle", g, 0, o, r) for o in range(2) for r in range(4)]
        got = [] if lv == 0 else [("two", g, 0, o, r) for o in range(2) for r in (1, 2, 3)]
        sent = [("ag", g, lv, 0, d, h) for h in range(PIECES) for d in range(2)]
        steps["solve", g, lv] = (after, got, sent)
        for step in (1, 2, 3):
            for h in range(PIECES):
                for d in range(2):
                    if h in goes(step, d):
                        steps["ag", g, lv, step, d, h] = (
                            [("ag", g, lv, step, d, h - 1) if h - 1 in goes(step, d)
                             else ("solve", g, lv)],
                            [("ag", g, lv, step - 1, d, h)],
                            [("ag", g, lv, step, d, h)],
                        )
        last = [("ag", g, lv, 3, d, h) for d in range(2) for h in goes(3, d)]
        last += [
            ("ag", g, lv, 2, d, h) for d in range(2) for h in range(PIECES) if h not in goes(3, d)
        ]
        for n in range(4):
            before = [("theirs", g, lv, n - 1)] if n else [
                ("ag", g, lv, step, d, h)
                for step in (1, 2, 3) for d in range(2) for h in goes(step, d)
            ]
            steps["theirs", g, lv, n] = (before, [] if n else last, [("pair", g, lv, n)])
        where = {}
        for n in range(4):
            sent = []
            for row in GROUPS[n]:
                where[row] = n
                for o in range(2):
                    main, r = (row[0], row[1]) if o == 0 else (row[1], row[0])
                    for d in range(2):
                        if main == 2 and r in VIA[d]:
                            sent.append(("far", g, lv, o, d, r))
                        if main == NEAR[d] and r not in VIA[d]:
                            sent.append(("near", g, lv, o, d, r))
            before = [("theirs", g, lv, n)] + ([("ours", g, lv, n - 1)] if n else [])
            steps["ours", g, lv, n] = (before, [("pair", g, lv, n)], sent)
        for o in range(2):
            for d in range(2):
                for r in VIA[d]:
                    row = (NEAR[d], r) if o == 0 else (r, NEAR[d])
                    steps["relay", g, lv, o, d, r] = (
                        [("ours", g, lv, where[row])],
                        [("far", g, lv, o, d, r)],
                        [("near", g, lv, o, d, r)],
                    )
            for r in range(4):
                row = (0, r) if o == 0 else (r, 0)
                steps["settle", g, lv, o, r] = (
                    [("ours", g, lv, where[row])],
                    [("near", g, lv, o, d, r) for d in range(2)],
                    [("two", g, lv, o, r)] if r else [],
                )
    steps["solve", g, 2] = (
        [("settle", g, 1, o, r) for o in range(2) for r in range(4)],
        [("two", g, 1, o, r) for o in range(2) for r in (1, 2, 3)],
        [],
    )
    return steps


def messages():
    return {
        name: at
        for at, name in enumerate(m for g in range(CHUNKS) for s in plan(g).values() for m in s[2])
    }


def kernel(
    cols_hbm, live_hbm, b_hbm, d_hbm, l_hbm, out_hbm,
    cols, live, out, lv_ref, bv, dv, xs, ps, pr, sums, far, near, mid, two, resid,
    in_sem, out_sem, ssem, rsem, credit,
):
    z = lax.axis_index("prow")
    x = lax.axis_index("pcol_0")
    y = lax.axis_index("pcol_1")
    c = lax.axis_index("pcol_2")
    mate = 1 - c
    grid = ("pcol_0", "pcol_1")
    mesh_id = pl.DeviceIdType.MESH

    here = {"prow": z, "pcol_0": x, "pcol_1": y, "pcol_2": c}
    turned = {
        axis: [value] + [lax.rem(value + k, size) for k in range(1, size)]
        for axis, value, size in (("prow", z, NZ), ("pcol_0", x, 4), ("pcol_1", y, 4))
    }

    def turn(axis, step):
        return turned[axis][step % len(turned[axis])]

    def at_device(axis, value):
        return tuple(value if name == axis else here[name] for name in here)

    loads = {}

    def load(name, src, dst):
        loads[name] = pltpu.make_async_copy(src, dst, in_sem.at[len(loads)])
        loads[name].start()

    load("d", d_hbm, dv)
    load("b0", b_hbm.at[0], bv.at[0])
    load("cols", cols_hbm, cols)
    load("live", live_hbm, live)
    load("l0", l_hbm.at[0], lv_ref.at[0])
    load("b1", b_hbm.at[1], bv.at[1])
    load("b2", b_hbm.at[2], bv.at[2])
    load("l1", l_hbm.at[1], lv_ref.at[1])

    barrier = pltpu.get_barrier_semaphore()
    friends = [at_device("pcol_2", mate)]
    friends += [at_device(axis, turn(axis, step)) for axis in grid for step in (1, 2, 3)]
    friends += [at_device("prow", turn("prow", sign)) for sign in SIGN]
    for friend in friends:
        pl.semaphore_signal(barrier, inc=1, device_id=friend, device_id_type=mesh_id)

    number = messages()
    copies = {}
    stored, writes = [], []

    def half(lv, g, o, main, r):
        rx, ry = (main, r) if o == 0 else (r, main)
        return sums.at[lv, g, rx, ry, pl.ds(o * HALF, HALF)]

    def ends(name):
        kind, g, lv = name[:3]
        if kind == "ag":
            step, d, h = name[3:]
            slot = xs[g].at[
                lv * NZ + turn("prow", -SIGN[d] * step), pl.ds(h * PIECE, PIECE)
            ]
            return slot, slot, at_device("prow", turn("prow", SIGN[d]))
        if kind == "pair":
            n = name[3]
            return ps.at[lv, g, n], pr.at[lv, g, n], at_device("pcol_2", mate)
        if kind == "two":
            o, r = name[3:]
            axis = grid[1 - o]
            friend = at_device(axis, turn(axis, r))
            return mid.at[lv, g, o, r], two.at[lv, g, o, r - 1], friend
        o, d, r = name[3:]
        axis = grid[o]
        friend = at_device(axis, turn(axis, SIGN[d]))
        if kind == "far":
            return half(lv, g, o, 2, r), far.at[lv, g, o, d, VIA[d].index(r)], friend
        return half(lv, g, o, NEAR[d], r), near.at[lv, g, o, d, r], friend

    def send(name):
        src, dst, friend = ends(name)
        at = number[name]
        copies[name] = pltpu.make_async_remote_copy(
            src_ref=src, dst_ref=dst, send_sem=ssem.at[at], recv_sem=rsem.at[at],
            device_id=friend, device_id_type=mesh_id,
        )
        copies[name].start()

    def row_total(g, lv, q):
        lefts, rights = [], []
        for k in range(SLOTS):
            v = cols[lv * SLOTS + k, 0, q]
            at = (v >> 8) * NZ + ((v & 255) >> 5)
            rights.append(xs[g][jnp.where(k < live[lv, q], at, 2 * NZ)])
            lefts.append(lv_ref[lv, q, k])
        return jnp.dot(
            jnp.concatenate(lefts, axis=1), jnp.concatenate(rights, axis=0),
            preferred_element_type=jnp.float32,
        )

    def row_of(row, core):
        return (turn("pcol_0", row[0]) * 4 + turn("pcol_1", row[1])) * 2 + core

    def f32(value):
        return value.astype(jnp.float32)

    def need_load(name):
        if loads[name] is not None:
            loads[name].wait()
            loads[name] = None

    def do(name):
        kind, g, lv = name[:3]
        if kind == "solve":
            here = pl.ds(g * W, W)
            if lv == 0:
                right = bv[0, 0, 0, :, here]
                xs[g][2 * NZ] = jnp.zeros((B, W), jnp.bfloat16)
            else:
                need_load("b%d" % lv)
                for o in range(2):
                    total = f32(mid[lv - 1, g, o, 0])
                    for r in range(3):
                        total = total + f32(two[lv - 1, g, o, r])
                    rows = pl.ds(o * HALF, HALF)
                    resid[g, rows] = (f32(bv[lv, 0, 0, rows, here]) - total).astype(jnp.bfloat16)
                right = resid[g]
            answer = jnp.dot(
                dv[lv, 0, 0], right, preferred_element_type=jnp.float32
            ).astype(jnp.bfloat16)
            out[lv, 0, 0, :, here] = answer
            stored.append(lv)
            if stored.count(lv) == CHUNKS:
                writes.append(pltpu.make_async_copy(out.at[lv], out_hbm.at[lv], out_sem.at[lv]))
                writes[-1].start()
            if lv < 2:
                xs[g][lv * NZ + z] = answer
            if lv == 0 and "barrier" not in loads:
                loads["barrier"] = None
                pl.semaphore_wait(barrier, len(friends))
            if lv == 1:
                for i in range(2):
                    pl.semaphore_wait(credit.at[g, i], 1)
        elif kind == "theirs":
            for need in ("cols", "live", "l%d" % lv):
                need_load(need)
            n = name[3]
            for i, row in enumerate(GROUPS[n]):
                ps[lv, g, n, i] = row_total(g, lv, row_of(row, mate)).astype(jnp.bfloat16)
        elif kind == "ours":
            n = name[3]
            for i, row in enumerate(GROUPS[n]):
                total = row_total(g, lv, row_of(row, c)) + f32(pr[lv, g, n, i])
                sums[lv, g, row[0], row[1]] = total.astype(jnp.bfloat16)
            if n == 3 and lv == 0:
                for i, sign in enumerate(SIGN):
                    pl.semaphore_signal(
                        credit.at[g, i], inc=1, device_id_type=mesh_id,
                        device_id=at_device("prow", turn("prow", sign)),
                    )
        elif kind == "relay":
            o, d, r = name[3:]
            mine = half(lv, g, o, NEAR[d], r)
            mine[...] = mine[...] + far[lv, g, o, d, VIA[d].index(r)]
        elif kind == "settle":
            o, r = name[3:]
            total = f32(half(lv, g, o, 0, r)[...])
            total = total + f32(near[lv, g, o, 0, r]) + f32(near[lv, g, o, 1, r])
            mid[lv, g, o, r] = total.astype(jnp.bfloat16)

    loads["d"].wait()
    loads["b0"].wait()
    steps = {}
    for g in range(CHUNKS):
        steps.update(plan(g))
    names = list(steps)
    for at in ORDER:
        name = names[at]
        for message in steps[name][1]:
            copies[message].wait_recv()
        do(name)
        for message in steps[name][2]:
            send(message)
    for copy in copies.values():
        copy.wait_send()
    for write in writes:
        write.wait()


def shards(b_panels, diag_inverse, l_blocks, block_cols, live_counts):
    any_spec = pl.BlockSpec(memory_space=pl.ANY)
    bf16 = jnp.bfloat16
    count = len(messages())
    return pl.pallas_call(
        kernel,
        name="front",
        out_shape=jax.ShapeDtypeStruct(b_panels.shape, bf16),
        in_specs=[any_spec] * 5,
        out_specs=any_spec,
        scratch_shapes=[
            pltpu.SMEM((2 * SLOTS, 1, 32), jnp.int32),
            pltpu.SMEM((2, 32), jnp.int32),
            pltpu.VMEM(b_panels.shape, bf16),
            pltpu.VMEM((2, 32, SLOTS, B, B), bf16),
            pltpu.VMEM(b_panels.shape, bf16),
            pltpu.VMEM(diag_inverse.shape, bf16),
            [pltpu.VMEM((2 * NZ + 1, B, W), bf16) for _ in range(CHUNKS)],
            pltpu.VMEM((2, CHUNKS, 4, 4, B, W), bf16),
            pltpu.VMEM((2, CHUNKS, 4, 4, B, W), bf16),
            pltpu.VMEM((2, CHUNKS, 4, 4, B, W), bf16),
            pltpu.VMEM((2, CHUNKS, 2, 2, 2, HALF, W), bf16),
            pltpu.VMEM((2, CHUNKS, 2, 2, 4, HALF, W), bf16),
            pltpu.VMEM((2, CHUNKS, 2, 4, HALF, W), bf16),
            pltpu.VMEM((2, CHUNKS, 2, 3, HALF, W), bf16),
            pltpu.VMEM((CHUNKS, B, W), bf16),
            pltpu.SemaphoreType.DMA((8,)),
            pltpu.SemaphoreType.DMA((3,)),
            pltpu.SemaphoreType.DMA((count,)),
            pltpu.SemaphoreType.DMA((count,)),
            pltpu.SemaphoreType.REGULAR((CHUNKS, 2)),
        ],
        compiler_params=pltpu.CompilerParams(
            collective_id=0, has_side_effects=True, vmem_limit_bytes=60 * 2**20
        ),
    )(
        block_cols.transpose(0, 1, 4, 2, 3).reshape(2 * SLOTS, 1, 32),
        live_counts.reshape(2, 32),
        b_panels,
        diag_inverse,
        l_blocks.reshape(2, 32, SLOTS, B, B),
    )


def solution(mesh):
    finer = Mesh(
        mesh.devices.reshape(mesh.shape["prow"], 4, 4, 2), ("prow", "pcol_0", "pcol_1", "pcol_2")
    )
    return jax.shard_map(
        shards,
        mesh=finer,
        in_specs=(
            P(None, "prow", PCOL, None, None),
            P(None, "prow", PCOL, None, None),
            P(None, "prow", PCOL, None, None, None, None),
            P(None, "prow", PCOL, None, None),
            P(None, "prow", PCOL, None),
        ),
        out_specs=P(None, "prow", PCOL, None, None),
        check_vma=False,
    )
```

```python
import functools

import jax
import jax.numpy as jnp
from jax import lax
from jax.experimental import pallas as pl
from jax.experimental.pallas import tpu as pltpu
from jax.sharding import Mesh
from jax.sharding import PartitionSpec as P

PCOL = ("pcol_0", "pcol_1", "pcol_2")
CHUNKS = 2
B = 128
RHS = 512
W = RHS // CHUNKS
SLOTS = 5
NZ = 8
HALF = B // 2
PIECES = 2
PIECE = B // PIECES
SIGN = (1, -1)
NEAR = (1, 3)
VIA = ((2, 1), (0, 3))
GROUPS = (
    ((2, 2), (2, 0), (0, 2), (2, 1)),
    ((1, 2), (2, 3), (3, 2), (1, 1)),
    ((3, 3), (1, 3), (3, 1), (1, 0)),
    ((0, 1), (3, 0), (0, 3), (0, 0)),
)
ORDER = (
    0, 71, 2, 1, 4, 3, 73, 72, 75, 74, 6, 5, 8, 7, 77, 76, 79, 78, 9, 10, 80, 81, 11, 12, 13,
    82, 83, 15, 16, 86, 87, 84, 17, 27, 19, 14, 20, 28, 22, 30, 88, 98, 90, 85, 91, 99, 93, 101,
    25, 33, 18, 21, 29, 32, 24, 26, 34, 104, 96, 89, 92, 100, 103, 95, 97, 105, 23, 31, 35, 94,
    102, 106, 37, 36, 39, 38, 108, 107, 110, 109, 41, 40, 43, 42, 112, 111, 114, 113, 44, 45,
    115, 116, 46, 47, 48, 117, 118, 50, 51, 121, 122, 119, 62, 52, 54, 49, 55, 63, 57, 65, 133,
    125, 123, 120, 126, 134, 128, 136, 60, 68, 53, 56, 64, 67, 59, 61, 69, 131, 139, 124, 127,
    135, 138, 130, 132, 140, 58, 66, 70, 129, 137, 141,
)


def goes(step, d):
    if step < 3:
        return tuple(range(PIECES))
    return tuple(h for h in range(PIECES) if h * 2 // PIECES == d)


def plan(g):
    steps = {}
    for lv in range(2):
        after = [] if lv == 0 else [("settle", g, 0, o, r) for o in range(2) for r in range(4)]
        got = [] if lv == 0 else [("two", g, 0, o, r) for o in range(2) for r in (1, 2, 3)]
        sent = [("ag", g, lv, 0, d, h) for h in range(PIECES) for d in range(2)]
        steps["solve", g, lv] = (after, got, sent)
        for step in (1, 2, 3):
            for h in range(PIECES):
                for d in range(2):
                    if h in goes(step, d):
                        steps["ag", g, lv, step, d, h] = (
                            [("ag", g, lv, step, d, h - 1) if h - 1 in goes(step, d)
                             else ("solve", g, lv)],
                            [("ag", g, lv, step - 1, d, h)],
                            [("ag", g, lv, step, d, h)],
                        )
        last = [("ag", g, lv, 3, d, h) for d in range(2) for h in goes(3, d)]
        last += [
            ("ag", g, lv, 2, d, h) for d in range(2) for h in range(PIECES) if h not in goes(3, d)
        ]
        for n in range(4):
            before = [("theirs", g, lv, n - 1)] if n else [
                ("ag", g, lv, step, d, h)
                for step in (1, 2, 3) for d in range(2) for h in goes(step, d)
            ]
            steps["theirs", g, lv, n] = (before, [] if n else last, [("pair", g, lv, n)])
        where = {}
        for n in range(4):
            sent = []
            for row in GROUPS[n]:
                where[row] = n
                for o in range(2):
                    main, r = (row[0], row[1]) if o == 0 else (row[1], row[0])
                    for d in range(2):
                        if main == 2 and r in VIA[d]:
                            sent.append(("far", g, lv, o, d, r))
                        if main == NEAR[d] and r not in VIA[d]:
                            sent.append(("near", g, lv, o, d, r))
            before = [("theirs", g, lv, n)] + ([("ours", g, lv, n - 1)] if n else [])
            steps["ours", g, lv, n] = (before, [("pair", g, lv, n)], sent)
        for o in range(2):
            for d in range(2):
                for r in VIA[d]:
                    row = (NEAR[d], r) if o == 0 else (r, NEAR[d])
                    steps["relay", g, lv, o, d, r] = (
                        [("ours", g, lv, where[row])],
                        [("far", g, lv, o, d, r)],
                        [("near", g, lv, o, d, r)],
                    )
            for r in range(4):
                row = (0, r) if o == 0 else (r, 0)
                steps["settle", g, lv, o, r] = (
                    [("ours", g, lv, where[row])],
                    [("near", g, lv, o, d, r) for d in range(2)],
                    [("two", g, lv, o, r)] if r else [],
                )
    steps["solve", g, 2] = (
        [("settle", g, 1, o, r) for o in range(2) for r in range(4)],
        [("two", g, 1, o, r) for o in range(2) for r in (1, 2, 3)],
        [],
    )
    return steps


def messages():
    return {
        name: at
        for at, name in enumerate(m for g in range(CHUNKS) for s in plan(g).values() for m in s[2])
    }


def kernel(
    cols_hbm, live_hbm, b_hbm, d_hbm, l_hbm, out_hbm,
    cols, live, out, lv_ref, bv, dv, xs, ps, pr, sums, far, near, mid, two, resid,
    in_sem, out_sem, ssem, rsem, credit,
):
    z = lax.axis_index("prow")
    x = lax.axis_index("pcol_0")
    y = lax.axis_index("pcol_1")
    c = lax.axis_index("pcol_2")
    mate = 1 - c
    grid = ("pcol_0", "pcol_1")
    mesh_id = pl.DeviceIdType.MESH

    here = {"prow": z, "pcol_0": x, "pcol_1": y, "pcol_2": c}
    turned = {
        axis: [value] + [lax.rem(value + k, size) for k in range(1, size)]
        for axis, value, size in (("prow", z, NZ), ("pcol_0", x, 4), ("pcol_1", y, 4))
    }

    def turn(axis, step):
        return turned[axis][step % len(turned[axis])]

    def at_device(axis, value):
        return tuple(value if name == axis else here[name] for name in here)

    loads = {}

    def load(name, src, dst):
        loads[name] = pltpu.make_async_copy(src, dst, in_sem.at[len(loads)])
        loads[name].start()

    load("d", d_hbm, dv)
    load("b0", b_hbm.at[0], bv.at[0])
    load("cols", cols_hbm, cols)
    load("live", live_hbm, live)
    load("l0", l_hbm.at[0], lv_ref.at[0])
    load("b1", b_hbm.at[1], bv.at[1])
    load("b2", b_hbm.at[2], bv.at[2])
    load("l1", l_hbm.at[1], lv_ref.at[1])

    barrier = pltpu.get_barrier_semaphore()
    friends = [at_device("pcol_2", mate)]
    friends += [at_device(axis, turn(axis, step)) for axis in grid for step in (1, 2, 3)]
    friends += [at_device("prow", turn("prow", sign)) for sign in SIGN]
    for friend in friends:
        pl.semaphore_signal(barrier, inc=1, device_id=friend, device_id_type=mesh_id)

    number = messages()
    copies = {}
    stored, writes = [], []

    def half(lv, g, o, main, r):
        rx, ry = (main, r) if o == 0 else (r, main)
        return sums.at[lv, g, rx, ry, pl.ds(o * HALF, HALF)]

    def ends(name):
        kind, g, lv = name[:3]
        if kind == "ag":
            step, d, h = name[3:]
            slot = xs[g].at[
                lv * NZ + turn("prow", -SIGN[d] * step), pl.ds(h * PIECE, PIECE)
            ]
            return slot, slot, at_device("prow", turn("prow", SIGN[d]))
        if kind == "pair":
            n = name[3]
            return ps.at[lv, g, n], pr.at[lv, g, n], at_device("pcol_2", mate)
        if kind == "two":
            o, r = name[3:]
            axis = grid[1 - o]
            friend = at_device(axis, turn(axis, r))
            return mid.at[lv, g, o, r], two.at[lv, g, o, r - 1], friend
        o, d, r = name[3:]
        axis = grid[o]
        friend = at_device(axis, turn(axis, SIGN[d]))
        if kind == "far":
            return half(lv, g, o, 2, r), far.at[lv, g, o, d, VIA[d].index(r)], friend
        return half(lv, g, o, NEAR[d], r), near.at[lv, g, o, d, r], friend

    def send(name):
        src, dst, friend = ends(name)
        at = number[name]
        copies[name] = pltpu.make_async_remote_copy(
            src_ref=src, dst_ref=dst, send_sem=ssem.at[at], recv_sem=rsem.at[at],
            device_id=friend, device_id_type=mesh_id,
        )
        copies[name].start()

    def row_total(g, lv, q):
        lefts, rights = [], []
        for k in range(SLOTS):
            v = cols[lv * SLOTS + k, 0, q]
            at = (v >> 8) * NZ + ((v & 255) >> 5)
            rights.append(xs[g][jnp.where(k < live[lv, q], at, 2 * NZ)])
            lefts.append(lv_ref[lv, q, k])
        return jnp.dot(
            jnp.concatenate(lefts, axis=1), jnp.concatenate(rights, axis=0),
            preferred_element_type=jnp.float32,
        )

    def row_of(row, core):
        return (turn("pcol_0", row[0]) * 4 + turn("pcol_1", row[1])) * 2 + core

    def f32(value):
        return value.astype(jnp.float32)

    def need_load(name):
        if loads[name] is not None:
            loads[name].wait()
            loads[name] = None

    def do(name):
        kind, g, lv = name[:3]
        if kind == "solve":
            here = pl.ds(g * W, W)
            if lv == 0:
                right = bv[0, 0, 0, :, here]
                xs[g][2 * NZ] = jnp.zeros((B, W), jnp.bfloat16)
            else:
                need_load("b%d" % lv)
                for o in range(2):
                    total = f32(mid[lv - 1, g, o, 0])
                    for r in range(3):
                        total = total + f32(two[lv - 1, g, o, r])
                    rows = pl.ds(o * HALF, HALF)
                    resid[g, rows] = (f32(bv[lv, 0, 0, rows, here]) - total).astype(jnp.bfloat16)
                right = resid[g]
            answer = jnp.dot(
                dv[lv, 0, 0], right, preferred_element_type=jnp.float32
            ).astype(jnp.bfloat16)
            out[lv, 0, 0, :, here] = answer
            stored.append(lv)
            if stored.count(lv) == CHUNKS:
                writes.append(pltpu.make_async_copy(out.at[lv], out_hbm.at[lv], out_sem.at[lv]))
                writes[-1].start()
            if lv < 2:
                xs[g][lv * NZ + z] = answer
            if lv == 0 and "barrier" not in loads:
                loads["barrier"] = None
                pl.semaphore_wait(barrier, len(friends))
            if lv == 1:
                for i in range(2):
                    pl.semaphore_wait(credit.at[g, i], 1)
        elif kind == "theirs":
            for need in ("cols", "live", "l%d" % lv):
                need_load(need)
            n = name[3]
            for i, row in enumerate(GROUPS[n]):
                ps[lv, g, n, i] = row_total(g, lv, row_of(row, mate)).astype(jnp.bfloat16)
        elif kind == "ours":
            n = name[3]
            for i, row in enumerate(GROUPS[n]):
                total = row_total(g, lv, row_of(row, c)) + f32(pr[lv, g, n, i])
                sums[lv, g, row[0], row[1]] = total.astype(jnp.bfloat16)
            if n == 3 and lv == 0:
                for i, sign in enumerate(SIGN):
                    pl.semaphore_signal(
                        credit.at[g, i], inc=1, device_id_type=mesh_id,
                        device_id=at_device("prow", turn("prow", sign)),
                    )
        elif kind == "relay":
            o, d, r = name[3:]
            mine = half(lv, g, o, NEAR[d], r)
            mine[...] = mine[...] + far[lv, g, o, d, VIA[d].index(r)]
        elif kind == "settle":
            o, r = name[3:]
            total = f32(half(lv, g, o, 0, r)[...])
            total = total + f32(near[lv, g, o, 0, r]) + f32(near[lv, g, o, 1, r])
            mid[lv, g, o, r] = total.astype(jnp.bfloat16)

    loads["d"].wait()
    loads["b0"].wait()
    steps = {}
    for g in range(CHUNKS):
        steps.update(plan(g))
    names = list(steps)
    for at in ORDER:
        name = names[at]
        for message in steps[name][1]:
            copies[message].wait_recv()
        do(name)
        for message in steps[name][2]:
            send(message)
    for copy in copies.values():
        copy.wait_send()
    for write in writes:
        write.wait()


def shards(b_panels, diag_inverse, l_blocks, block_cols, live_counts):
    any_spec = pl.BlockSpec(memory_space=pl.ANY)
    bf16 = jnp.bfloat16
    count = len(messages())
    return pl.pallas_call(
        kernel,
        name="front",
        out_shape=jax.ShapeDtypeStruct(b_panels.shape, bf16),
        in_specs=[any_spec] * 5,
        out_specs=any_spec,
        scratch_shapes=[
            pltpu.SMEM((2 * SLOTS, 1, 32), jnp.int32),
            pltpu.SMEM((2, 32), jnp.int32),
            pltpu.VMEM(b_panels.shape, bf16),
            pltpu.VMEM((2, 32, SLOTS, B, B), bf16),
            pltpu.VMEM(b_panels.shape, bf16),
            pltpu.VMEM(diag_inverse.shape, bf16),
            [pltpu.VMEM((2 * NZ + 1, B, W), bf16) for _ in range(CHUNKS)],
            pltpu.VMEM((2, CHUNKS, 4, 4, B, W), bf16),
            pltpu.VMEM((2, CHUNKS, 4, 4, B, W), bf16),
            pltpu.VMEM((2, CHUNKS, 4, 4, B, W), bf16),
            pltpu.VMEM((2, CHUNKS, 2, 2, 2, HALF, W), bf16),
            pltpu.VMEM((2, CHUNKS, 2, 2, 4, HALF, W), bf16),
            pltpu.VMEM((2, CHUNKS, 2, 4, HALF, W), bf16),
            pltpu.VMEM((2, CHUNKS, 2, 3, HALF, W), bf16),
            pltpu.VMEM((CHUNKS, B, W), bf16),
            pltpu.SemaphoreType.DMA((8,)),
            pltpu.SemaphoreType.DMA((3,)),
            pltpu.SemaphoreType.DMA((count,)),
            pltpu.SemaphoreType.DMA((count,)),
            pltpu.SemaphoreType.REGULAR((CHUNKS, 2)),
        ],
        compiler_params=pltpu.CompilerParams(
            collective_id=0, has_side_effects=True, vmem_limit_bytes=60 * 2**20
        ),
    )(
        block_cols.transpose(0, 1, 4, 2, 3).reshape(2 * SLOTS, 1, 32),
        live_counts.reshape(2, 32),
        b_panels,
        diag_inverse,
        l_blocks.reshape(2, 32, SLOTS, B, B),
    )


def solution(mesh):
    finer = Mesh(
        mesh.devices.reshape(mesh.shape["prow"], 4, 4, 2), ("prow", "pcol_0", "pcol_1", "pcol_2")
    )
    return jax.shard_map(
        shards,
        mesh=finer,
        in_specs=(
            P(None, "prow", PCOL, None, None),
            P(None, "prow", PCOL, None, None),
            P(None, "prow", PCOL, None, None, None, None),
            P(None, "prow", PCOL, None, None),
            P(None, "prow", PCOL, None),
        ),
        out_specs=P(None, "prow", PCOL, None, None),
        check_vma=False,
    )
```
